128 devices in a mesh: blk: 8 (over x, y_lo), elem: 16 (over y_hi, z, core).
Axes of the slice: x: 4, y: 4 (y_hi: 2, y_lo: 2; y = y_hi * 2 + y_lo), z: 4, core: 2. Of those that a mesh axis runs over, the one named last changes fastest.
Arguments:
- state: float32 [512, 125, 32, 128], P('blk', None, 'elem'), may hold values from -18 to 18
- rhs: float32 [512, 125, 32, 128], P('blk', None, 'elem'), may hold values from -6 to 6
- to_modal: float32 [125, 125], replicated, may hold values from -1 to 2
- viscous_op: float32 [125, 125], replicated, may hold values from -0.5 to 0.5
- sweep_gain: float32 [512, 125, 125], P('blk'), may hold values from -1 to 1.2
- inv_blocks: float32 [512, 125, 125], P('blk'), may hold values from -0.125 to 0.125
Outputs:
- line_solution: float32 [512, 125, 32, 128], P(('blk', 'elem'))
The draws below stay inside these ranges and needn't reach their ends.
All inputs are finite; a program needn't handle non-finite values.
Results may differ from the reference program's by a relative error of at most 0.0003.
Values sent between devices are 32-bit elements; how exact they have to be, the bound alone decides.
A program may use at most 128 MiB of HBM per device.

```python
import math
import jax
import jax.numpy as jnp
from jax import lax

ORDER = 4
NODES = 125
AX = 128
NAZ = 512
RAD = 32


def draw_state(key, part):
    first, second = jax.random.split(key)
    base = jnp.clip(jax.random.normal(first, (NAZ, NODES, RAD, AX), jnp.float32), -6.0, 6.0)
    spread = jnp.exp(jax.random.uniform(second, (NAZ, 1, RAD, AX), jnp.float32, math.log(0.1), math.log(3.0)))
    nodeid = jnp.arange(NODES).reshape(1, NODES, 1, 1)
    return base * jnp.where(nodeid >= ORDER ** 3, spread, 1.0)


def draw_to_modal(key, part):
    noise = jnp.clip(jax.random.normal(key, (NODES, NODES), jnp.float32), -6.0, 6.0)
    return jnp.eye(NODES, dtype=jnp.float32) + 0.3 / math.sqrt(NODES) * noise


def draw_sweep_gain(key, part):
    first, second, third, fourth, fifth, sixth = jax.random.split(jax.random.fold_in(key, 7), 6)
    upper = math.log(0.1)
    rates = jnp.exp(jax.random.uniform(first, (1, NODES, 1), jnp.float32, math.log(0.5 / NAZ), upper))
    factor = jax.random.uniform(second, (NAZ, 1, 1), jnp.float32, 0.5, 1.5)
    diagonal = jnp.exp(-rates * factor)
    order_nodes = jax.random.permutation(fourth, NODES).astype(jnp.int32)
    position = jnp.argsort(order_nodes).astype(jnp.int32)
    parity = position % 2
    mate_position = position + 1 - 2 * parity
    paired = mate_position < NODES
    mate_position = jnp.where(paired, mate_position, position)
    partner = order_nodes[mate_position]
    magnitude = jax.random.uniform(fifth, (NAZ, NODES), jnp.float32, 0.3, 1.2)
    turn_sign = jnp.where(jax.random.uniform(sixth, (NAZ, NODES), jnp.float32) < 0.5, -1.0, 1.0)
    pair_angle = (magnitude * turn_sign)[:, position // 2]
    pair_angle = jnp.where(paired[None, :], pair_angle, 0.0)
    row_sign = jnp.where(parity == 0, 1.0, -1.0).astype(jnp.float32)
    columns = jnp.arange(NODES).reshape(1, 1, NODES)
    rows = jnp.arange(NODES).reshape(1, NODES, 1)
    on_self = (columns == rows).astype(jnp.float32)
    on_mate = (columns == partner.reshape(1, NODES, 1)).astype(jnp.float32) * (1.0 - on_self)
    rotation = jnp.cos(pair_angle)[:, :, None] * on_self + (row_sign[None, :] * jnp.sin(pair_angle))[:, :, None] * on_mate
    noise = jnp.clip(jax.random.normal(third, (NAZ, NODES, NODES), jnp.float32), -4.0, 4.0)
    return 0.02 / math.sqrt(NODES) * noise + diagonal * rotation


def shard_levels(stream_key, shape, shards, low, largest):
    loudness = 1.0
    for dim, blocks in shards:
        steps = jax.random.uniform(jax.random.fold_in(jax.random.fold_in(stream_key, 6), dim), (blocks,), jnp.float32, low / len(shards), largest / len(shards))
        loudness = loudness * jnp.repeat(jnp.exp(steps), shape[dim] // blocks).reshape((-1,) + (1,) * (len(shape) - 1 - dim))
    return loudness


def gaussian(rng, shape, deviation, limit, shards=(), kind=jnp.bfloat16):
    array = jax.random.normal(rng, shape, jnp.float32) * deviation
    if len(shards) > 0:
        array = shard_levels(rng, shape, shards, -0.22, 0.18) * array
    return jnp.clip(array, min=-limit, max=limit).astype(kind)


def setup_inputs(seed: int = 0) -> dict:
    arg_keys = jax.random.split(jax.random.key(seed), 7)
    state = draw_state(jax.random.fold_in(arg_keys[6], 71), 0)
    rhs = gaussian(arg_keys[1], (NAZ, NODES, RAD, AX), 1.0, 6.0, ((0, 8), (2, 16)), jnp.float32)
    to_modal = draw_to_modal(jax.random.fold_in(arg_keys[6], 71), 0)
    viscous_op = gaussian(arg_keys[3], (NODES, NODES), NODES ** -0.5, 0.5, (), jnp.float32)
    sweep_gain = draw_sweep_gain(jax.random.fold_in(arg_keys[6], 71), 0)
    inv_blocks = gaussian(arg_keys[5], (NAZ, NODES, NODES), (NODES * 16) ** -0.5, 0.125, ((0, 8),), jnp.float32)
    return dict(state=state, rhs=rhs, to_modal=to_modal, viscous_op=viscous_op, sweep_gain=sweep_gain, inv_blocks=inv_blocks)


def reference(state, rhs, to_modal, viscous_op, sweep_gain, inv_blocks):
    highest = lax.Precision.HIGHEST
    modal = jnp.einsum('mn,knja->kmja', to_modal, state, precision=highest)
    squares = modal * modal
    upper = jnp.sum(squares[:, ORDER ** 3:], axis=1) / NODES
    energy = jnp.mean(squares, axis=1) + 1e-6
    sensor = upper / energy
    padded = jnp.pad(sensor, ((0, 0), (1, 1), (0, 0)))
    smooth = (4.0 * sensor + jnp.roll(sensor, 1, 0) + jnp.roll(sensor, -1, 0) + padded[:, 2:] + padded[:, :-2]) / 8.0
    viscous = jnp.einsum('mn,knja->kmja', viscous_op, state, precision=highest)
    force = rhs + smooth[:, None] * viscous
    coupled = jnp.einsum('kmn,knja->kmja', inv_blocks, force, precision=highest)

    def sweep_step(field, inputs):
        matrix, source = inputs
        field = jnp.einsum('mn,nja->mja', matrix, field, precision=highest) + source
        return field, field

    start = jnp.zeros(coupled.shape[1:], jnp.float32)
    cycle_end, _ = lax.scan(sweep_step, start, (sweep_gain, coupled))
    _, solved = lax.scan(sweep_step, cycle_end, (sweep_gain, coupled))
    return solved
```

```python
import functools

import jax
import jax.numpy as jnp
from jax import lax
from jax.experimental import pallas as pl
from jax.experimental.pallas import tpu as pltpu
from jax.sharding import PartitionSpec as P

ORDER = 4
NODES = 125
LOCAL = 64
CHUNK = 4
PAD = 128
MESH = pl.DeviceIdType.MESH
F32 = jnp.float32
BF16 = jnp.bfloat16


def halves(x):
    high = x.astype(BF16)
    return high, (x - high.astype(F32)).astype(BF16)


def as_rows(x):
    high, low = halves(x)
    return jnp.concatenate(
        [
            jnp.concatenate([high, high], axis=1),
            jnp.concatenate([low, low], axis=1),
        ],
        axis=0,
    )


def stacked(y):
    high, low = halves(y)
    return jnp.concatenate([high, low], axis=0)


def product(rows, columns):
    both = jnp.dot(rows, columns, preferred_element_type=F32)
    half = both.shape[0] // 2
    return both[:half] + both[half:]


def block_of(ref, k):
    part = ref[pl.ds(k, PAD, stride=LOCAL), :]
    return jnp.concatenate([part, jnp.zeros((PAD, PAD - NODES), F32)], axis=1)


def field_of(ref, k):
    start = k * (2 * NODES)
    return jnp.concatenate(
        [
            ref[pl.ds(start, PAD, stride=2), :],
            ref[pl.ds(start + 1, PAD, stride=2), :],
        ],
        axis=1,
    )


def main_kernel(
    state_h,
    rhs_h,
    modal_ref,
    visc_ref,
    gain_h,
    inv_h,
    rc_h,
    ru_h,
    gl_ref,
    st,
    rh,
    gs,
    iv,
    padm,
    tv,
    vx,
    c,
    sens,
    edge,
    hk,
    hj,
    sm,
    z,
    p4,
    m4,
    zb,
    xb,
    u,
    load_sem,
    hk_send,
    hk_recv,
    hj_send,
    hj_recv,
    c_send,
    c_recv,
    u_send,
    u_recv,
    z_sem,
    x_send,
    x_recv,
    own_sem,
):
    b = lax.axis_index("blk")
    e = lax.axis_index("elem")
    nb = lax.axis_size("blk")
    ne = lax.axis_size("elem")
    bx = b // 2
    bl = b % 2
    rows = 2 * NODES * LOCAL
    pieces = 4
    piece = rows // pieces

    loads = []
    for i in range(pieces):
        part = pl.ds(i * piece, piece)
        loads.append(pltpu.make_async_copy(state_h.at[part], st.at[part], load_sem.at[i]))
    loads.append(pltpu.make_async_copy(rhs_h, rh.at[pl.ds(0, rows)], load_sem.at[4]))
    block_rows = NODES * LOCAL
    loads.append(pltpu.make_async_copy(inv_h, iv.at[pl.ds(0, block_rows)], load_sem.at[5]))
    loads.append(pltpu.make_async_copy(gain_h, gs.at[pl.ds(0, block_rows)], load_sem.at[6]))
    for load in loads:
        load.start()

    barrier = pltpu.get_barrier_semaphore()

    def greet(i, carry):
        pl.semaphore_signal(barrier, inc=1, device_id={"elem": (e + i) % ne}, device_id_type=MESH)
        return carry

    lax.fori_loop(1, ne, greet, 0)
    for d in (1, 2, 4, 6, 7):
        pl.semaphore_signal(barrier, inc=1, device_id={"blk": (b + d) % nb}, device_id_type=MESH)

    st[pl.ds(rows, 8), :] = jnp.zeros((8, PAD), F32)
    rh[pl.ds(rows, 8), :] = jnp.zeros((8, PAD), F32)
    tail = (PAD - NODES) * LOCAL
    gs[pl.ds(block_rows, tail), :] = jnp.zeros((tail, NODES), F32)
    iv[pl.ds(block_rows, tail), :] = jnp.zeros((tail, NODES), F32)

    padm[...] = jnp.zeros((2, PAD, PAD), F32)
    padm[0, 0:NODES, 0:NODES] = modal_ref[...]
    padm[1, 0:NODES, 0:NODES] = visc_ref[...]
    for i in range(2):
        made = as_rows(padm[i])
        tv[pl.ds(i * PAD, PAD), :] = made[:PAD]
        tv[pl.ds((i + 2) * PAD, PAD), :] = made[PAD:]

    def sense(k, carry):
        both = product(tv[...], stacked(field_of(st, k)))
        vx[k] = both[PAD:]
        squares = both[:PAD] * both[:PAD]
        low = jnp.sum(squares[: ORDER**3], axis=0, keepdims=True)
        upper = jnp.sum(squares[ORDER**3 :], axis=0, keepdims=True)
        value = (upper / NODES) / ((low + upper) / NODES + 1e-6)
        sens[0, pl.ds(k, 1), :] = value[:, :PAD]
        sens[1, pl.ds(k, 1), :] = value[:, PAD:]
        return carry

    for i in range(pieces):
        loads[i].wait()
        if i < pieces - 1:
            last = LOCAL // pieces * (i + 1) - 1
            first = LOCAL // pieces * i - (1 if i else 0)
            lax.fori_loop(first, last, sense, 0)
        else:
            lax.fori_loop(LOCAL // pieces * i - 1, LOCAL, sense, 0)

    for j in range(2):
        edge[0, j : j + 1, :] = sens[j, 0:1, :]
        edge[1, j : j + 1, :] = sens[j, LOCAL - 1 : LOCAL, :]
    pl.semaphore_wait(barrier, ne - 1 + 5)

    to_next = pltpu.make_async_remote_copy(
        edge.at[1], hk.at[0], hk_send.at[0], hk_recv.at[0],
        device_id={"blk": (b + 1) % nb}, device_id_type=MESH,
    )
    to_last = pltpu.make_async_remote_copy(
        edge.at[0], hk.at[1], hk_send.at[1], hk_recv.at[1],
        device_id={"blk": (b + nb - 1) % nb}, device_id_type=MESH,
    )
    outer = pltpu.make_async_remote_copy(
        sens.at[1], hj.at[0], hj_send.at[0], hj_recv.at[0],
        device_id={"elem": (e + 1) % ne}, device_id_type=MESH,
    )
    inner = pltpu.make_async_remote_copy(
        sens.at[0], hj.at[1], hj_send.at[1], hj_recv.at[1],
        device_id={"elem": (e + ne - 1) % ne}, device_id_type=MESH,
    )
    for copy in (to_next, to_last, outer, inner):
        copy.start()
    for copy in (to_next, to_last, outer, inner):
        copy.wait()
    has_inner = jnp.where(e > 0, 1.0, 0.0).astype(F32)
    has_outer = jnp.where(e < ne - 1, 1.0, 0.0).astype(F32)
    beside = (hj[0] * has_inner, sens[0], sens[1], hj[1] * has_outer)
    for j in range(2):
        here = sens[j]
        before = jnp.concatenate([hk[0, j : j + 1, :], here[:-1]], axis=0)
        after = jnp.concatenate([here[1:], hk[1, j : j + 1, :]], axis=0)
        sm[j] = (4.0 * here + after + before + beside[j + 2] + beside[j]) / 8.0

    loads[4].wait()
    loads[5].wait()

    def force_one(k):
        scale = jnp.concatenate(
            [
                jnp.broadcast_to(sm[0, pl.ds(k, 1), :], (PAD, PAD)),
                jnp.broadcast_to(sm[1, pl.ds(k, 1), :], (PAD, PAD)),
            ],
            axis=1,
        )
        force = field_of(rh, k) + scale * vx[k]
        coupled = product(as_rows(block_of(iv, k)), stacked(force))
        c[k, 0] = coupled[:, :PAD]
        c[k, 1] = coupled[:, PAD:]

    def early(to):
        return pltpu.make_async_remote_copy(
            c.at[pl.ds(CHUNK * to + 1, CHUNK - 1)], rc_h.at[e], c_send.at[to], c_recv.at[e],
            device_id={"elem": to}, device_id_type=MESH,
        )

    def forcing(i, carry):
        to = (e + i) % ne

        def one(r, inner_carry):
            force_one(CHUNK * to + r)
            return inner_carry

        lax.fori_loop(0, CHUNK, one, 0, unroll=True)
        early(to).start()
        return carry

    lax.fori_loop(1, ne, forcing, 0)
    for r in range(CHUNK):
        force_one(CHUNK * e + r)
    own_c = pltpu.make_async_copy(
        c.at[pl.ds(CHUNK * e + 1, CHUNK - 1)], rc_h.at[e], own_sem.at[0]
    )
    own_c.start()

    loads[6].wait()
    row = lax.broadcasted_iota(jnp.int32, (PAD, PAD), 0)
    column = lax.broadcasted_iota(jnp.int32, (PAD, PAD), 1)
    z[:, pl.ds(0, 2 * PAD)] = jnp.zeros((PAD, 2 * PAD), F32)
    z[:, pl.ds(2 * PAD, PAD)] = jnp.where((row == column) & (row < NODES), 1.0, 0.0).astype(F32)

    def sweep(k):
        made = product(as_rows(block_of(gs, k)), stacked(z[...]))
        z[:, pl.ds(0, PAD)] = made[:, :PAD] + c[k, 0]
        z[:, pl.ds(PAD, PAD)] = made[:, PAD : 2 * PAD] + c[k, 1]
        z[:, pl.ds(2 * PAD, PAD)] = made[:, 2 * PAD :]

    def sweeps(i, carry):
        for r in range(CHUNK):
            sweep(CHUNK * i + r)
            if r == 0:
                p4[i] = z[:, pl.ds(0, 2 * PAD)]
                m4[i] = as_rows(z[:, pl.ds(2 * PAD, PAD)])
        return carry

    lax.fori_loop(0, LOCAL // CHUNK, sweeps, 0)

    zb[bl] = z[...]
    pair = pltpu.make_async_remote_copy(
        zb.at[bl], zb.at[bl], z_sem.at[0], z_sem.at[1],
        device_id={"blk": b + 1 - 2 * bl}, device_id_type=MESH,
    )
    pair.start()
    for i in range(CHUNK - 1):
        gl_ref[i] = as_rows(block_of(gs, CHUNK * e + 1 + i))
    pair.wait()

    def advance(ref, at, field):
        return product(as_rows(ref[at, :, pl.ds(2 * PAD, PAD)]), stacked(field))

    made = advance(zb, 1, zb[0])
    xb[bx, :, pl.ds(0, 2 * PAD)] = made[:, : 2 * PAD] + zb[1, :, pl.ds(0, 2 * PAD)]
    xb[bx, :, pl.ds(2 * PAD, PAD)] = made[:, 2 * PAD :]
    ring = nb // 2

    def along(i):
        return pltpu.make_async_remote_copy(
            xb.at[bx], xb.at[bx], x_send.at[i], x_recv.at[i],
            device_id={"blk": (b + 2 * i) % nb}, device_id_type=MESH,
        )

    for i in range(1, ring):
        along(i).start()
    for i in range(1, ring):
        along(i).wait()

    field = z.at[:, pl.ds(0, 2 * PAD)]
    field[...] = jnp.zeros((PAD, 2 * PAD), F32)

    def pass_pair(i, carry):
        at = i % ring
        field[...] = advance(xb, at, field[...]) + xb[at, :, pl.ds(0, 2 * PAD)]
        return carry

    lax.fori_loop(0, ring + bx, pass_pair, 0)

    @pl.when(bl == 1)
    def _():
        field[...] = advance(zb, 0, field[...]) + zb[0, :, pl.ds(0, 2 * PAD)]

    z_start = m4.at[0]
    start = stacked(field[...])

    def late(to):
        return pltpu.make_async_remote_copy(
            u.at[to], ru_h.at[e], u_send.at[to], u_recv.at[e],
            device_id={"elem": to}, device_id_type=MESH,
        )

    def first_field(to):
        made = product(m4[to], start) + p4[to]
        u[to, 0] = made[:, :PAD]
        u[to, 1] = made[:, PAD:]

    def first_fields(i, carry):
        to = (e + i) % ne
        first_field(to)
        late(to).start()
        return carry

    lax.fori_loop(1, ne, first_fields, 0)
    first_field(e)
    own_u = pltpu.make_async_copy(u.at[e], ru_h.at[e], own_sem.at[1])
    own_u.start()
    own_c.wait()
    own_u.wait()

    def finish(i, carry):
        to = (e + i) % ne
        source = (e + ne - i) % ne
        early(to).wait_send()
        late(to).wait_send()
        pltpu.make_async_remote_copy(
            c.at[pl.ds(CHUNK * to + 1, CHUNK - 1)], rc_h.at[source], c_send.at[to],
            c_recv.at[source], device_id={"elem": to}, device_id_type=MESH,
        ).wait_recv()
        pltpu.make_async_remote_copy(
            u.at[to], ru_h.at[source], u_send.at[to], u_recv.at[source],
            device_id={"elem": to}, device_id_type=MESH,
        ).wait_recv()
        return carry

    lax.fori_loop(1, ne, finish, 0)


def last_kernel(gl_ref, rc_ref, ru_ref, out_ref):
    out = out_ref.reshape(CHUNK * NODES * 8, PAD)
    sources = ru_ref.shape[0]
    pairs = [(s, j) for s in range(sources) for j in range(2)]

    def put(r, field):
        for i in range(len(pairs)):
            out[pl.ds(r * NODES * 8 + i, NODES, stride=8), :] = field[
                :NODES, i * PAD : (i + 1) * PAD
            ]

    field = jnp.concatenate([ru_ref[s, j] for s, j in pairs], axis=1)
    put(0, field)
    for r in range(CHUNK - 1):
        source = jnp.concatenate([rc_ref[s, r, j] for s, j in pairs], axis=1)
        field = product(gl_ref[r], stacked(field)) + source
        put(r + 1, field)


def body(state, rhs, to_modal, viscous_op, sweep_gain, inv_blocks):
    ne = lax.axis_size("elem")
    rows = LOCAL * NODES * 2
    flat = lambda x: x.reshape(rows, PAD)
    blocks = lambda x: jnp.transpose(x, (1, 0, 2)).reshape(NODES * LOCAL, NODES)
    vmem, dma = pltpu.VMEM, pltpu.SemaphoreType.DMA
    anywhere = pl.BlockSpec(memory_space=pl.ANY)
    local = pl.BlockSpec(memory_space=pltpu.VMEM)
    rc, ru, gl = pl.pallas_call(
        main_kernel,
        out_shape=(
            jax.ShapeDtypeStruct((ne, CHUNK - 1, 2, PAD, PAD), F32),
            jax.ShapeDtypeStruct((ne, 2, PAD, PAD), F32),
            jax.ShapeDtypeStruct((CHUNK - 1, 2 * PAD, 2 * PAD), BF16),
        ),
        in_specs=[anywhere, anywhere, local, local, anywhere, anywhere],
        out_specs=(anywhere, anywhere, local),
        scratch_shapes=[
            vmem((rows + 8, PAD), F32),
            vmem((rows + 8, PAD), F32),
            vmem((PAD * LOCAL, NODES), F32),
            vmem((PAD * LOCAL, NODES), F32),
            vmem((2, PAD, PAD), F32),
            vmem((4 * PAD, 2 * PAD), BF16),
            vmem((LOCAL, PAD, 2 * PAD), F32),
            vmem((LOCAL, 2, PAD, PAD), F32),
            vmem((2, LOCAL, PAD), F32),
            vmem((2, 8, PAD), F32),
            vmem((2, 8, PAD), F32),
            vmem((2, LOCAL, PAD), F32),
            vmem((2, LOCAL, PAD), F32),
            vmem((PAD, 3 * PAD), F32),
            vmem((LOCAL // CHUNK, PAD, 2 * PAD), F32),
            vmem((LOCAL // CHUNK, 2 * PAD, 2 * PAD), BF16),
            vmem((2, PAD, 3 * PAD), F32),
            vmem((4, PAD, 3 * PAD), F32),
            vmem((LOCAL // CHUNK, 2, PAD, PAD), F32),
            dma((7,)),
            dma((2,)),
            dma((2,)),
            dma((2,)),
            dma((2,)),
            dma((16,)),
            dma((16,)),
            dma((16,)),
            dma((16,)),
            dma((2,)),
            dma((4,)),
            dma((4,)),
            dma((2,)),
        ],
        compiler_params=pltpu.CompilerParams(
            collective_id=0, has_side_effects=True, vmem_limit_bytes=62 * 2**20
        ),
        name="line_main",
    )(flat(state), flat(rhs), to_modal, viscous_op, blocks(sweep_gain), blocks(inv_blocks))
    out = pl.pallas_call(
        last_kernel,
        grid=(4,),
        out_shape=jax.ShapeDtypeStruct((CHUNK * NODES, 2 * ne, PAD), F32),
        in_specs=[
            pl.BlockSpec((CHUNK - 1, 2 * PAD, 2 * PAD), lambda i: (0, 0, 0)),
            pl.BlockSpec((4, CHUNK - 1, 2, PAD, PAD), lambda i: (i, 0, 0, 0, 0)),
            pl.BlockSpec((4, 2, PAD, PAD), lambda i: (i, 0, 0, 0)),
        ],
        out_specs=pl.BlockSpec((CHUNK * NODES, 8, PAD), lambda i: (0, i, 0)),
        compiler_params=pltpu.CompilerParams(vmem_limit_bytes=48 * 2**20),
        name="line_last",
    )(gl, rc, ru)
    return out.reshape(CHUNK, NODES, 2 * ne, PAD)


def solution(mesh):
    in_specs = (
        P("blk", None, "elem", None),
        P("blk", None, "elem", None),
        P(),
        P(),
        P("blk", None, None),
        P("blk", None, None),
    )
    out_specs = P(("blk", "elem"), None, None, None)
    return jax.shard_map(body, mesh=mesh, in_specs=in_specs, out_specs=out_specs, check_vma=False)
```

```python
import functools

import jax
import jax.numpy as jnp
from jax import lax
from jax.experimental import pallas as pl
from jax.experimental.pallas import tpu as pltpu
from jax.sharding import PartitionSpec as P

ORDER = 4
NODES = 125
LOCAL = 64
CHUNK = 4
PAD = 128
PART = 8
UNROLL = 4
HOLD = 4
MESH = pl.DeviceIdType.MESH
F32 = jnp.float32
BF16 = jnp.bfloat16


def halves(x):
    high = x.astype(BF16)
    return high, (x - high.astype(F32)).astype(BF16)


def as_rows(x):
    high, low = halves(x)
    return jnp.concatenate([high, high, low], axis=1)


def stacked(y):
    high, low = halves(y)
    return jnp.concatenate([high, low, high], axis=0)


def product(rows, columns):
    return jnp.dot(rows, columns, preferred_element_type=F32)


def block_of(ref, k):
    part = ref[pl.ds(k, PAD, stride=LOCAL), :]
    return jnp.concatenate([part, jnp.zeros((PAD, PAD - NODES), F32)], axis=1)


def field_at(ref, start):
    return jnp.concatenate(
        [
            ref[pl.ds(start, PAD, stride=2), :],
            ref[pl.ds(start + 1, PAD, stride=2), :],
        ],
        axis=1,
    )


def main_kernel(
    state_h,
    rhs_h,
    modal_ref,
    visc_ref,
    gain_h,
    inv_h,
    rc_h,
    ru_h,
    gl_ref,
    st,
    rh,
    gs,
    iv,
    padm,
    tv,
    vx,
    c,
    sens,
    edge,
    hk,
    hj,
    sm,
    z,
    p4,
    m4,
    zb,
    xb,
    u,
    load_sem,
    st_sem,
    rh_sem,
    hk_send,
    hk_recv,
    hj_send,
    hj_recv,
    c_send,
    c_recv,
    u_send,
    u_recv,
    z_sem,
    x_send,
    x_recv,
    own_sem,
):
    b = lax.axis_index("blk")
    e = lax.axis_index("elem")
    nb = lax.axis_size("blk")
    ne = lax.axis_size("elem")
    bx = b // 2
    bl = b % 2
    parts = LOCAL // PART
    part_rows = 2 * NODES * PART
    block_rows = NODES * LOCAL

    def load_part(source, target, sem, p):
        first = pl.multiple_of(p * part_rows, 8)
        return pltpu.make_async_copy(
            source.at[pl.ds(first, part_rows)], target.at[p, pl.ds(0, part_rows)], sem.at[p]
        )

    load_inv = pltpu.make_async_copy(inv_h, iv.at[pl.ds(0, block_rows)], load_sem.at[0])
    load_gain = pltpu.make_async_copy(gain_h, gs.at[pl.ds(0, block_rows)], load_sem.at[1])
    for p in range(parts):
        load_part(state_h, st, st_sem, p).start()
    for p in range(parts):
        load_part(rhs_h, rh, rh_sem, p).start()
    load_inv.start()
    load_gain.start()

    barrier = pltpu.get_barrier_semaphore()

    def greet(i, carry):
        pl.semaphore_signal(barrier, inc=1, device_id={"elem": (e + i) % ne}, device_id_type=MESH)
        return carry

    lax.fori_loop(1, ne, greet, 0)
    for d in (1, 2, 4, 6, 7):
        pl.semaphore_signal(barrier, inc=1, device_id={"blk": (b + d) % nb}, device_id_type=MESH)

    for p in range(parts):
        st[p, pl.ds(part_rows, 8), :] = jnp.zeros((8, PAD), F32)
        rh[p, pl.ds(part_rows, 8), :] = jnp.zeros((8, PAD), F32)
    tail = (PAD - NODES) * LOCAL
    gs[pl.ds(block_rows, tail), :] = jnp.zeros((tail, NODES), F32)
    iv[pl.ds(block_rows, tail), :] = jnp.zeros((tail, NODES), F32)

    padm[...] = jnp.zeros((2, PAD, PAD), F32)
    padm[0, 0:NODES, 0:NODES] = modal_ref[...]
    padm[1, 0:NODES, 0:NODES] = visc_ref[...]
    for i in range(2):
        tv[pl.ds(i * PAD, PAD), :] = as_rows(padm[i])

    def sense(source, within, k):
        both = product(tv[...], stacked(field_at(source, 2 * NODES * within)))
        vx[k] = both[PAD:]
        squares = both[:PAD] * both[:PAD]
        low = jnp.sum(squares[: ORDER**3], axis=0, keepdims=True)
        upper = jnp.sum(squares[ORDER**3 :], axis=0, keepdims=True)
        value = (upper / NODES) / ((low + upper) / NODES + 1e-6)
        sens[0, pl.ds(k, 1), :] = value[:, :PAD]
        sens[1, pl.ds(k, 1), :] = value[:, PAD:]

    def sense_part(p, carry):
        load_part(state_h, st, st_sem, p).wait()

        def some(i, inner_carry):
            for r in range(UNROLL):
                sense(st.at[p], UNROLL * i + r, PART * p + UNROLL * i + r)
            return inner_carry

        lax.fori_loop(0, PART // UNROLL, some, 0)
        return carry

    lax.fori_loop(0, parts, sense_part, 0)
    for j in range(2):
        edge[0, j : j + 1, :] = sens[j, 0:1, :]
        edge[1, j : j + 1, :] = sens[j, LOCAL - 1 : LOCAL, :]
    pl.semaphore_wait(barrier, ne - 1 + 5)

    to_next = pltpu.make_async_remote_copy(
        edge.at[1], hk.at[0], hk_send.at[0], hk_recv.at[0],
        device_id={"blk": (b + 1) % nb}, device_id_type=MESH,
    )
    to_last = pltpu.make_async_remote_copy(
        edge.at[0], hk.at[1], hk_send.at[1], hk_recv.at[1],
        device_id={"blk": (b + nb - 1) % nb}, device_id_type=MESH,
    )
    outer = pltpu.make_async_remote_copy(
        sens.at[1], hj.at[0], hj_send.at[0], hj_recv.at[0],
        device_id={"elem": (e + 1) % ne}, device_id_type=MESH,
    )
    inner = pltpu.make_async_remote_copy(
        sens.at[0], hj.at[1], hj_send.at[1], hj_recv.at[1],
        device_id={"elem": (e + ne - 1) % ne}, device_id_type=MESH,
    )
    for copy in (outer, inner, to_next, to_last):
        copy.start()
    for copy in (outer, inner, to_next, to_last):
        copy.wait_recv()
    has_inner = jnp.where(e > 0, 1.0, 0.0).astype(F32)
    has_outer = jnp.where(e < ne - 1, 1.0, 0.0).astype(F32)
    beside = (hj[0] * has_inner, sens[0], sens[1], hj[1] * has_outer)
    for j in range(2):
        here = sens[j]
        before = jnp.concatenate([hk[0, j : j + 1, :], here[:-1]], axis=0)
        after = jnp.concatenate([here[1:], hk[1, j : j + 1, :]], axis=0)
        sm[j] = (4.0 * here + after + before + beside[j + 2] + beside[j]) / 8.0

    load_inv.wait()

    def wait_rhs(p, carry):
        load_part(rhs_h, rh, rh_sem, p).wait()
        return carry

    lax.fori_loop(0, parts, wait_rhs, 0)

    def force_one(k):
        scale = jnp.concatenate(
            [
                jnp.broadcast_to(sm[0, pl.ds(k, 1), :], (PAD, PAD)),
                jnp.broadcast_to(sm[1, pl.ds(k, 1), :], (PAD, PAD)),
            ],
            axis=1,
        )
        force = field_at(rh.at[k // PART], 2 * NODES * (k % PART)) + scale * vx[k]
        coupled = product(as_rows(block_of(iv, k)), stacked(force))
        c[k, 0] = coupled[:, :PAD]
        c[k, 1] = coupled[:, PAD:]

    def early(to):
        return pltpu.make_async_remote_copy(
            c.at[pl.ds(CHUNK * to + 1, CHUNK - 1)], rc_h.at[e], c_send.at[to], c_recv.at[e],
            device_id={"elem": to}, device_id_type=MESH,
        )

    side = ne // 2
    mine = side * (e // side)

    def near(d):
        return mine + (e + d) % side

    def far(d):
        return side - mine + (e + d) % side

    def forcing(to):
        for r in range(CHUNK):
            force_one(CHUNK * to + r)

    def force_both(d, carry):
        forcing(far(d))
        early(far(d)).start()
        forcing(near(d + 1))
        early(near(d + 1)).start()
        return carry

    def force_near(d, carry):
        forcing(near(d))
        early(near(d)).start()
        return carry

    def force_far(d, carry):
        forcing(far(d))
        return carry

    def send_far(d, carry):
        early(far(d)).start()
        return carry

    lax.fori_loop(0, HOLD, force_both, 0)
    lax.fori_loop(HOLD + 1, side, force_near, 0)
    lax.fori_loop(HOLD, side, force_far, 0)
    for r in range(CHUNK):
        force_one(CHUNK * e + r)
    own_c = pltpu.make_async_copy(
        c.at[pl.ds(CHUNK * e + 1, CHUNK - 1)], rc_h.at[e], own_sem.at[0]
    )
    own_c.start()

    load_gain.wait()
    row = lax.broadcasted_iota(jnp.int32, (PAD, PAD), 0)
    column = lax.broadcasted_iota(jnp.int32, (PAD, PAD), 1)
    z[:, pl.ds(0, 2 * PAD)] = jnp.zeros((PAD, 2 * PAD), F32)
    z[:, pl.ds(2 * PAD, PAD)] = jnp.where((row == column) & (row < NODES), 1.0, 0.0).astype(F32)

    def sweep(k):
        made = product(as_rows(block_of(gs, k)), stacked(z[...]))
        z[:, pl.ds(0, PAD)] = made[:, :PAD] + c[k, 0]
        z[:, pl.ds(PAD, PAD)] = made[:, PAD : 2 * PAD] + c[k, 1]
        z[:, pl.ds(2 * PAD, PAD)] = made[:, 2 * PAD :]

    def sweeps(i, carry):
        for r in range(CHUNK):
            sweep(CHUNK * i + r)
            if r == 0:
                p4[i] = z[:, pl.ds(0, 2 * PAD)]
                m4[i] = as_rows(z[:, pl.ds(2 * PAD, PAD)])
        return carry

    lax.fori_loop(0, LOCAL // CHUNK, sweeps, 0)

    zb[bl] = z[...]
    pair = pltpu.make_async_remote_copy(
        zb.at[bl], zb.at[bl], z_sem.at[0], z_sem.at[1],
        device_id={"blk": b + 1 - 2 * bl}, device_id_type=MESH,
    )
    pair.start()
    lax.fori_loop(HOLD, side, send_far, 0)
    for i in range(CHUNK - 1):
        gl_ref[i] = as_rows(block_of(gs, CHUNK * e + 1 + i))
    pair.wait()

    def advance(ref, at, field):
        return product(as_rows(ref[at, :, pl.ds(2 * PAD, PAD)]), stacked(field))

    made = advance(zb, 1, zb[0])
    xb[bx, :, pl.ds(0, 2 * PAD)] = made[:, : 2 * PAD] + zb[1, :, pl.ds(0, 2 * PAD)]
    xb[bx, :, pl.ds(2 * PAD, PAD)] = made[:, 2 * PAD :]
    ring = nb // 2

    def along(i):
        return pltpu.make_async_remote_copy(
            xb.at[bx], xb.at[bx], x_send.at[i], x_recv.at[i],
            device_id={"blk": (b + 2 * i) % nb}, device_id_type=MESH,
        )

    for i in range(1, ring):
        along(i).start()
    for i in range(1, ring):
        along(i).wait()

    field = z.at[:, pl.ds(0, 2 * PAD)]
    field[...] = jnp.zeros((PAD, 2 * PAD), F32)

    def pass_pair(i, carry):
        at = i % ring
        field[...] = advance(xb, at, field[...]) + xb[at, :, pl.ds(0, 2 * PAD)]
        return carry

    lax.fori_loop(0, ring + bx, pass_pair, 0)

    @pl.when(bl == 1)
    def _():
        field[...] = advance(zb, 0, field[...]) + zb[0, :, pl.ds(0, 2 * PAD)]

    start = stacked(field[...])

    def late(to):
        return pltpu.make_async_remote_copy(
            u.at[to], ru_h.at[e], u_send.at[to], u_recv.at[e],
            device_id={"elem": to}, device_id_type=MESH,
        )

    def first_field(to):
        made = product(m4[to], start) + p4[to]
        u[to, 0] = made[:, :PAD]
        u[to, 1] = made[:, PAD:]

    def first_fields(i, carry):
        to = (e + i) % ne
        first_field(to)
        late(to).start()
        return carry

    lax.fori_loop(1, ne, first_fields, 0)
    first_field(e)
    own_u = pltpu.make_async_copy(u.at[e], ru_h.at[e], own_sem.at[1])
    own_u.start()
    own_c.wait()
    own_u.wait()

    for copy in (outer, inner, to_next, to_last):
        copy.wait_send()

    def finish(i, carry):
        to = (e + i) % ne
        source = (e + ne - i) % ne
        early(to).wait_send()
        late(to).wait_send()
        pltpu.make_async_remote_copy(
            c.at[pl.ds(CHUNK * to + 1, CHUNK - 1)], rc_h.at[source], c_send.at[to],
            c_recv.at[source], device_id={"elem": to}, device_id_type=MESH,
        ).wait_recv()
        pltpu.make_async_remote_copy(
            u.at[to], ru_h.at[source], u_send.at[to], u_recv.at[source],
            device_id={"elem": to}, device_id_type=MESH,
        ).wait_recv()
        return carry

    lax.fori_loop(1, ne, finish, 0)


def last_kernel(gl_ref, rc_ref, ru_ref, out_ref):
    out = out_ref.reshape(CHUNK * NODES * 8, PAD)
    sources = ru_ref.shape[0]
    pairs = [(s, j) for s in range(sources) for j in range(2)]

    def put(r, field):
        for i in range(len(pairs)):
            out[pl.ds(r * NODES * 8 + i, NODES, stride=8), :] = field[
                :NODES, i * PAD : (i + 1) * PAD
            ]

    field = jnp.concatenate([ru_ref[s, j] for s, j in pairs], axis=1)
    put(0, field)
    for r in range(CHUNK - 1):
        source = jnp.concatenate([rc_ref[s, r, j] for s, j in pairs], axis=1)
        field = product(gl_ref[r], stacked(field)) + source
        put(r + 1, field)


def body(state, rhs, to_modal, viscous_op, sweep_gain, inv_blocks):
    ne = lax.axis_size("elem")
    rows = LOCAL * NODES * 2
    parts = LOCAL // PART
    flat = lambda x: x.reshape(rows, PAD)
    blocks = lambda x: jnp.transpose(x, (1, 0, 2)).reshape(NODES * LOCAL, NODES)
    vmem, dma = pltpu.VMEM, pltpu.SemaphoreType.DMA
    anywhere = pl.BlockSpec(memory_space=pl.ANY)
    local = pl.BlockSpec(memory_space=pltpu.VMEM)
    rc, ru, gl = pl.pallas_call(
        main_kernel,
        out_shape=(
            jax.ShapeDtypeStruct((ne, CHUNK - 1, 2, PAD, PAD), F32),
            jax.ShapeDtypeStruct((ne, 2, PAD, PAD), F32),
            jax.ShapeDtypeStruct((CHUNK - 1, PAD, 3 * PAD), BF16),
        ),
        in_specs=[anywhere, anywhere, local, local, anywhere, anywhere],
        out_specs=(anywhere, anywhere, local),
        scratch_shapes=[
            vmem((parts, rows // parts + 8, PAD), F32),
            vmem((parts, rows // parts + 8, PAD), F32),
            vmem((PAD * LOCAL, NODES), F32),
            vmem((PAD * LOCAL, NODES), F32),
            vmem((2, PAD, PAD), F32),
            vmem((2 * PAD, 3 * PAD), BF16),
            vmem((LOCAL, PAD, 2 * PAD), F32),
            vmem((LOCAL, 2, PAD, PAD), F32),
            vmem((2, LOCAL, PAD), F32),
            vmem((2, 8, PAD), F32),
            vmem((2, 8, PAD), F32),
            vmem((2, LOCAL, PAD), F32),
            vmem((2, LOCAL, PAD), F32),
            vmem((PAD, 3 * PAD), F32),
            vmem((LOCAL // CHUNK, PAD, 2 * PAD), F32),
            vmem((LOCAL // CHUNK, PAD, 3 * PAD), BF16),
            vmem((2, PAD, 3 * PAD), F32),
            vmem((4, PAD, 3 * PAD), F32),
            vmem((LOCAL // CHUNK, 2, PAD, PAD), F32),
            dma((2,)),
            dma((parts,)),
            dma((parts,)),
            dma((2,)),
            dma((2,)),
            dma((2,)),
            dma((2,)),
            dma((16,)),
            dma((16,)),
            dma((16,)),
            dma((16,)),
            dma((2,)),
            dma((4,)),
            dma((4,)),
            dma((2,)),
        ],
        compiler_params=pltpu.CompilerParams(
            collective_id=0, has_side_effects=True, vmem_limit_bytes=62 * 2**20
        ),
        name="line_main",
    )(flat(state), flat(rhs), to_modal, viscous_op, blocks(sweep_gain), blocks(inv_blocks))
    out = pl.pallas_call(
        last_kernel,
        grid=(4,),
        out_shape=jax.ShapeDtypeStruct((CHUNK * NODES, 2 * ne, PAD), F32),
        in_specs=[
            pl.BlockSpec((CHUNK - 1, PAD, 3 * PAD), lambda i: (0, 0, 0)),
            pl.BlockSpec((4, CHUNK - 1, 2, PAD, PAD), lambda i: (i, 0, 0, 0, 0)),
            pl.BlockSpec((4, 2, PAD, PAD), lambda i: (i, 0, 0, 0)),
        ],
        out_specs=pl.BlockSpec((CHUNK * NODES, 8, PAD), lambda i: (0, i, 0)),
        compiler_params=pltpu.CompilerParams(vmem_limit_bytes=63 * 2**20),
        name="line_last",
    )(gl, rc, ru)
    return out.reshape(CHUNK, NODES, 2 * ne, PAD)


def solution(mesh):
    in_specs = (
        P("blk", None, "elem", None),
        P("blk", None, "elem", None),
        P(),
        P(),
        P("blk", None, None),
        P("blk", None, None),
    )
    out_specs = P(("blk", "elem"), None, None, None)
    return jax.shard_map(body, mesh=mesh, in_specs=in_specs, out_specs=out_specs, check_vma=False)
```

```python
import functools

import jax
import jax.numpy as jnp
from jax import lax
from jax.experimental import pallas as pl
from jax.experimental.pallas import tpu as pltpu
from jax.sharding import PartitionSpec as P

ORDER = 4
NODES = 125
LOCAL = 64
CHUNK = 4
PAD = 128
QUAD = 4
PART = 8
UNROLL = 4
HOLD = 4
MESH = pl.DeviceIdType.MESH
F32 = jnp.float32
BF16 = jnp.bfloat16


def halves(x):
    high = x.astype(BF16)
    return high, (x - high.astype(F32)).astype(BF16)


def as_rows(x):
    high, low = halves(x)
    return jnp.concatenate([high, high, low], axis=1)


def stacked(y):
    high, low = halves(y)
    return jnp.concatenate([high, low, high], axis=0)


def product(rows, columns):
    return jnp.dot(rows, columns, preferred_element_type=F32)


def block_of(ref, k):
    part = ref[pl.ds(k, PAD, stride=LOCAL), :]
    return jnp.concatenate([part, jnp.zeros((PAD, PAD - NODES), F32)], axis=1)


def field_at(ref, start):
    return jnp.concatenate(
        [
            ref[pl.ds(start, PAD, stride=2), :],
            ref[pl.ds(start + 1, PAD, stride=2), :],
        ],
        axis=1,
    )


def main_kernel(
    state_h,
    rhs_h,
    modal_ref,
    visc_ref,
    gain_h,
    inv_h,
    rc0_h,
    rc1_h,
    rc2_h,
    ru_h,
    gl_ref,
    st,
    rh,
    gs,
    iv,
    padm,
    tv,
    c,
    sens,
    edge,
    hk,
    hj,
    sm,
    z,
    p4,
    m4,
    zb,
    xb,
    u,
    load_sem,
    st_sem,
    rh_sem,
    hk_send,
    hk_recv,
    hj_send,
    hj_recv,
    c_send,
    c_recv,
    u_send,
    u_recv,
    z_sem,
    x_send,
    x_recv,
    own_sem,
):
    b = lax.axis_index("blk")
    e = lax.axis_index("elem")
    nb = lax.axis_size("blk")
    ne = lax.axis_size("elem")
    bx = b // 2
    bl = b % 2
    parts = LOCAL // PART
    part_rows = 2 * NODES * PART
    block_rows = NODES * LOCAL

    def load_part(source, target, sem, p):
        first = pl.multiple_of(p * part_rows, 8)
        return pltpu.make_async_copy(
            source.at[pl.ds(first, part_rows)], target.at[p, pl.ds(0, part_rows)], sem.at[p]
        )

    load_inv = pltpu.make_async_copy(inv_h, iv.at[pl.ds(0, block_rows)], load_sem.at[0])
    load_gain = pltpu.make_async_copy(gain_h, gs.at[pl.ds(0, block_rows)], load_sem.at[1])
    for p in range(parts):
        load_part(state_h, st, st_sem, p).start()
    for p in range(parts):
        load_part(rhs_h, rh, rh_sem, p).start()
    load_inv.start()
    load_gain.start()

    barrier = pltpu.get_barrier_semaphore()

    def greet(i, carry):
        pl.semaphore_signal(barrier, inc=1, device_id={"elem": (e + i) % ne}, device_id_type=MESH)
        return carry

    lax.fori_loop(1, ne, greet, 0)
    for d in (1, 2, 4, 6, 7):
        pl.semaphore_signal(barrier, inc=1, device_id={"blk": (b + d) % nb}, device_id_type=MESH)

    for p in range(parts):
        st[p, pl.ds(part_rows, 8), :] = jnp.zeros((8, PAD), F32)
        rh[p, pl.ds(part_rows, 8), :] = jnp.zeros((8, PAD), F32)
    tail = (PAD - NODES) * LOCAL
    gs[pl.ds(block_rows, tail), :] = jnp.zeros((tail, NODES), F32)
    iv[pl.ds(block_rows, tail), :] = jnp.zeros((tail, NODES), F32)

    padm[...] = jnp.zeros((2, PAD, PAD), F32)
    padm[0, 0:NODES, 0:NODES] = modal_ref[...]
    padm[1, 0:NODES, 0:NODES] = visc_ref[...]
    for i in range(2):
        tv[pl.ds(i * PAD, PAD), :] = as_rows(padm[i])

    def sense(source, within, k):
        both = product(tv[...], stacked(field_at(source, 2 * NODES * within)))
        c[k, 0] = both[PAD:, :PAD]
        c[k, 1] = both[PAD:, PAD:]
        squares = both[:PAD] * both[:PAD]
        low = jnp.sum(squares[: ORDER**3], axis=0, keepdims=True)
        upper = jnp.sum(squares[ORDER**3 :], axis=0, keepdims=True)
        value = (upper / NODES) / ((low + upper) / NODES + 1e-6)
        sens[0, pl.ds(k, 1), :] = value[:, :PAD]
        sens[1, pl.ds(k, 1), :] = value[:, PAD:]

    def sense_part(p, carry):
        load_part(state_h, st, st_sem, p).wait()

        def some(i, inner_carry):
            for r in range(UNROLL):
                sense(st.at[p], UNROLL * i + r, PART * p + UNROLL * i + r)
            return inner_carry

        lax.fori_loop(0, PART // UNROLL, some, 0)
        return carry

    lax.fori_loop(0, parts, sense_part, 0)
    for j in range(2):
        edge[0, j : j + 1, :] = sens[j, 0:1, :]
        edge[1, j : j + 1, :] = sens[j, LOCAL - 1 : LOCAL, :]
    pl.semaphore_wait(barrier, ne - 1 + 5)

    to_next = pltpu.make_async_remote_copy(
        edge.at[1], hk.at[0], hk_send.at[0], hk_recv.at[0],
        device_id={"blk": (b + 1) % nb}, device_id_type=MESH,
    )
    to_last = pltpu.make_async_remote_copy(
        edge.at[0], hk.at[1], hk_send.at[1], hk_recv.at[1],
        device_id={"blk": (b + nb - 1) % nb}, device_id_type=MESH,
    )
    outer = pltpu.make_async_remote_copy(
        sens.at[1], hj.at[0], hj_send.at[0], hj_recv.at[0],
        device_id={"elem": (e + 1) % ne}, device_id_type=MESH,
    )
    inner = pltpu.make_async_remote_copy(
        sens.at[0], hj.at[1], hj_send.at[1], hj_recv.at[1],
        device_id={"elem": (e + ne - 1) % ne}, device_id_type=MESH,
    )
    for copy in (outer, inner, to_next, to_last):
        copy.start()
    for copy in (outer, inner, to_next, to_last):
        copy.wait_recv()
    has_inner = jnp.where(e > 0, 1.0, 0.0).astype(F32)
    has_outer = jnp.where(e < ne - 1, 1.0, 0.0).astype(F32)
    beside = (hj[0] * has_inner, sens[0], sens[1], hj[1] * has_outer)
    for j in range(2):
        here = sens[j]
        before = jnp.concatenate([hk[0, j : j + 1, :], here[:-1]], axis=0)
        after = jnp.concatenate([here[1:], hk[1, j : j + 1, :]], axis=0)
        sm[j] = (4.0 * here + after + before + beside[j + 2] + beside[j]) / 8.0

    load_inv.wait()

    def wait_rhs(p, carry):
        load_part(rhs_h, rh, rh_sem, p).wait()
        return carry

    lax.fori_loop(0, parts, wait_rhs, 0)

    def force_one(k):
        scale = jnp.concatenate(
            [
                jnp.broadcast_to(sm[0, pl.ds(k, 1), :], (PAD, PAD)),
                jnp.broadcast_to(sm[1, pl.ds(k, 1), :], (PAD, PAD)),
            ],
            axis=1,
        )
        force = field_at(rh.at[k // PART], 2 * NODES * (k % PART)) + scale * jnp.concatenate([c[k, 0], c[k, 1]], axis=1)
        coupled = product(as_rows(block_of(iv, k)), stacked(force))
        c[k, 0] = coupled[:, :PAD]
        c[k, 1] = coupled[:, PAD:]

    rc_h = (rc0_h, rc1_h, rc2_h)

    def early_parts(to, source):
        return [
            pltpu.make_async_remote_copy(
                c.at[CHUNK * to + 1 + r], rc_h[r].at[source], c_send.at[r, to],
                c_recv.at[r, source], device_id={"elem": to}, device_id_type=MESH,
            )
            for r in range(CHUNK - 1)
        ]

    def early(to):
        for copy in early_parts(to, e):
            copy.start()

    side = ne // 2
    mine = side * (e // side)

    def near(d):
        return mine + (e + d) % side

    def far(d):
        return side - mine + (e + d) % side

    def forcing(to):
        for r in range(CHUNK):
            force_one(CHUNK * to + r)

    def force_both(d, carry):
        forcing(far(d))
        early(far(d))
        forcing(near(d + 1))
        early(near(d + 1))
        return carry

    def force_near(d, carry):
        forcing(near(d))
        early(near(d))
        return carry

    def force_far(d, carry):
        forcing(far(d))
        return carry

    def send_far(d, carry):
        early(far(d))
        return carry

    lax.fori_loop(0, HOLD, force_both, 0)
    lax.fori_loop(HOLD + 1, side, force_near, 0)
    lax.fori_loop(HOLD, side, force_far, 0)
    for r in range(CHUNK):
        force_one(CHUNK * e + r)
    own_c = [
        pltpu.make_async_copy(c.at[CHUNK * e + 1 + r], rc_h[r].at[e], own_sem.at[1 + r])
        for r in range(CHUNK - 1)
    ]
    for copy in own_c:
        copy.start()

    load_gain.wait()
    row = lax.broadcasted_iota(jnp.int32, (PAD, PAD), 0)
    column = lax.broadcasted_iota(jnp.int32, (PAD, PAD), 1)
    z[:, pl.ds(0, 2 * PAD)] = jnp.zeros((PAD, 2 * PAD), F32)
    z[:, pl.ds(2 * PAD, PAD)] = jnp.where((row == column) & (row < NODES), 1.0, 0.0).astype(F32)

    def sweep(k):
        made = product(as_rows(block_of(gs, k)), stacked(z[...]))
        z[:, pl.ds(0, PAD)] = made[:, :PAD] + c[k, 0]
        z[:, pl.ds(PAD, PAD)] = made[:, PAD : 2 * PAD] + c[k, 1]
        z[:, pl.ds(2 * PAD, PAD)] = made[:, 2 * PAD :]

    def sweeps(i, carry):
        for r in range(CHUNK):
            sweep(CHUNK * i + r)
            if r == 0:
                p4[i] = z[:, pl.ds(0, 2 * PAD)]
                m4[i] = as_rows(z[:, pl.ds(2 * PAD, PAD)])
        return carry

    lax.fori_loop(0, LOCAL // CHUNK, sweeps, 0)

    zb[bl] = z[...]
    pair = pltpu.make_async_remote_copy(
        zb.at[bl], zb.at[bl], z_sem.at[0], z_sem.at[1],
        device_id={"blk": b + 1 - 2 * bl}, device_id_type=MESH,
    )
    pair.start()
    lax.fori_loop(HOLD, side, send_far, 0)
    for i in range(CHUNK - 1):
        gl_ref[i] = as_rows(block_of(gs, CHUNK * e + 1 + i))
    pair.wait()

    def advance(ref, at, field):
        return product(as_rows(ref[at, :, pl.ds(2 * PAD, PAD)]), stacked(field))

    made = advance(zb, 1, zb[0])
    xb[bx, :, pl.ds(0, 2 * PAD)] = made[:, : 2 * PAD] + zb[1, :, pl.ds(0, 2 * PAD)]
    xb[bx, :, pl.ds(2 * PAD, PAD)] = made[:, 2 * PAD :]
    ring = nb // 2

    def along(i):
        return pltpu.make_async_remote_copy(
            xb.at[bx], xb.at[bx], x_send.at[i], x_recv.at[i],
            device_id={"blk": (b + 2 * i) % nb}, device_id_type=MESH,
        )

    for i in range(1, ring):
        along(i).start()
    for i in range(1, ring):
        along(i).wait()

    field = z.at[:, pl.ds(0, 2 * PAD)]
    field[...] = jnp.zeros((PAD, 2 * PAD), F32)

    def pass_pair(i, carry):
        at = i % ring
        field[...] = advance(xb, at, field[...]) + xb[at, :, pl.ds(0, 2 * PAD)]
        return carry

    lax.fori_loop(0, ring + bx, pass_pair, 0)

    @pl.when(bl == 1)
    def _():
        field[...] = advance(zb, 0, field[...]) + zb[0, :, pl.ds(0, 2 * PAD)]

    start = stacked(field[...])

    def late(to):
        return pltpu.make_async_remote_copy(
            u.at[to], ru_h.at[e], u_send.at[to], u_recv.at[e],
            device_id={"elem": to}, device_id_type=MESH,
        )

    def first_field(to):
        made = product(m4[to], start) + p4[to]
        u[to, 0] = made[:, :PAD]
        u[to, 1] = made[:, PAD:]

    def first_fields(i, carry):
        to = (e + i) % ne
        first_field(to)
        late(to).start()
        return carry

    lax.fori_loop(1, ne, first_fields, 0)
    first_field(e)
    own_u = pltpu.make_async_copy(u.at[e], ru_h.at[e], own_sem.at[0])
    own_u.start()
    for copy in own_c:
        copy.wait()
    own_u.wait()

    for copy in (outer, inner, to_next, to_last):
        copy.wait_send()

    def finish(i, carry):
        to = (e + i) % ne
        source = (e + ne - i) % ne
        late(to).wait_send()
        for copy in early_parts(to, e):
            copy.wait_send()
        for copy in early_parts(to, source):
            copy.wait_recv()
        pltpu.make_async_remote_copy(
            u.at[to], ru_h.at[source], u_send.at[to], u_recv.at[source],
            device_id={"elem": to}, device_id_type=MESH,
        ).wait_recv()
        return carry

    lax.fori_loop(1, ne, finish, 0)


def last_kernel(gl_ref, rc0_ref, rc1_ref, rc2_ref, ru_ref, out_ref):
    first = QUAD * pl.program_id(0)
    out = out_ref.reshape(CHUNK * NODES * 8, PAD)
    pairs = [(s, j) for s in range(QUAD) for j in range(2)]

    def put(r, field):
        for i in range(len(pairs)):
            out[pl.ds(r * NODES * 8 + i, NODES, stride=8), :] = field[
                :NODES, i * PAD : (i + 1) * PAD
            ]

    field = jnp.concatenate([ru_ref[first + s, j] for s, j in pairs], axis=1)
    put(0, field)
    for r, rc_ref in enumerate((rc0_ref, rc1_ref, rc2_ref)):
        source = jnp.concatenate([rc_ref[first + s, j] for s, j in pairs], axis=1)
        field = product(gl_ref[r], stacked(field)) + source
        put(r + 1, field)


def body(state, rhs, to_modal, viscous_op, sweep_gain, inv_blocks):
    ne = lax.axis_size("elem")
    rows = LOCAL * NODES * 2
    parts = LOCAL // PART
    flat = lambda x: x.reshape(rows, PAD)
    blocks = lambda x: jnp.transpose(x, (1, 0, 2)).reshape(NODES * LOCAL, NODES)
    vmem, dma = pltpu.VMEM, pltpu.SemaphoreType.DMA
    anywhere = pl.BlockSpec(memory_space=pl.ANY)
    far_memory = pl.BlockSpec(memory_space=pltpu.HBM)
    local = pl.BlockSpec(memory_space=pltpu.VMEM)
    blocks_in = jax.ShapeDtypeStruct((ne, 2, PAD, PAD), F32)
    rc0, rc1, rc2, ru, gl = pl.pallas_call(
        main_kernel,
        out_shape=(
            blocks_in,
            blocks_in,
            blocks_in,
            blocks_in,
            jax.ShapeDtypeStruct((CHUNK - 1, PAD, 3 * PAD), BF16),
        ),
        in_specs=[far_memory, far_memory, local, local, far_memory, far_memory],
        out_specs=(anywhere, anywhere, anywhere, anywhere, local),
        scratch_shapes=[
            vmem((parts, rows // parts + 8, PAD), F32),
            vmem((parts, rows // parts + 8, PAD), F32),
            vmem((PAD * LOCAL, NODES), F32),
            vmem((PAD * LOCAL, NODES), F32),
            vmem((2, PAD, PAD), F32),
            vmem((2 * PAD, 3 * PAD), BF16),
            vmem((LOCAL, 2, PAD, PAD), F32),
            vmem((2, LOCAL, PAD), F32),
            vmem((2, 8, PAD), F32),
            vmem((2, 8, PAD), F32),
            vmem((2, LOCAL, PAD), F32),
            vmem((2, LOCAL, PAD), F32),
            vmem((PAD, 3 * PAD), F32),
            vmem((LOCAL // CHUNK, PAD, 2 * PAD), F32),
            vmem((LOCAL // CHUNK, PAD, 3 * PAD), BF16),
            vmem((2, PAD, 3 * PAD), F32),
            vmem((4, PAD, 3 * PAD), F32),
            vmem((LOCAL // CHUNK, 2, PAD, PAD), F32),
            dma((2,)),
            dma((parts,)),
            dma((parts,)),
            dma((2,)),
            dma((2,)),
            dma((2,)),
            dma((2,)),
            dma((CHUNK - 1, 16)),
            dma((CHUNK - 1, 16)),
            dma((16,)),
            dma((16,)),
            dma((2,)),
            dma((4,)),
            dma((4,)),
            dma((CHUNK,)),
        ],
        compiler_params=pltpu.CompilerParams(
            collective_id=0, has_side_effects=True, vmem_limit_bytes=42 * 2**20
        ),
        name="line_main",
    )(flat(state), flat(rhs), to_modal, viscous_op, blocks(sweep_gain), blocks(inv_blocks))
    out = pl.pallas_call(
        last_kernel,
        grid=(ne // QUAD,),
        out_shape=jax.ShapeDtypeStruct((CHUNK * NODES, 2 * ne, PAD), F32),
        in_specs=[local] * 5,
        out_specs=pl.BlockSpec((CHUNK * NODES, 8, PAD), lambda i: (0, i, 0)),
        compiler_params=pltpu.CompilerParams(vmem_limit_bytes=40 * 2**20),
        name="line_last",
    )(gl, rc0, rc1, rc2, ru)
    return out.reshape(CHUNK, NODES, 2 * ne, PAD)


def solution(mesh):
    in_specs = (
        P("blk", None, "elem", None),
        P("blk", None, "elem", None),
        P(),
        P(),
        P("blk", None, None),
        P("blk", None, None),
    )
    out_specs = P(("blk", "elem"), None, None, None)
    return jax.shard_map(body, mesh=mesh, in_specs=in_specs, out_specs=out_specs, check_vma=False)
```

```python
import functools

import jax
import jax.numpy as jnp
from jax import lax
from jax.experimental import pallas as pl
from jax.experimental.pallas import tpu as pltpu
from jax.sharding import PartitionSpec as P

ORDER = 4
NODES = 125
LOCAL = 64
CHUNK = 4
PAD = 128
QUAD = 4
PART = 8
UNROLL = 4
HOLD = 4
MESH = pl.DeviceIdType.MESH
F32 = jnp.float32
BF16 = jnp.bfloat16


def halves(x):
    high = x.astype(BF16)
    return high, (x - high.astype(F32)).astype(BF16)


def as_rows(x):
    high, low = halves(x)
    return jnp.concatenate([high, high, low], axis=1)


def stacked(y):
    high, low = halves(y)
    return jnp.concatenate([high, low, high], axis=0)


def product(rows, columns):
    return jnp.dot(rows, columns, preferred_element_type=F32)


def block_of(ref, k):
    part = ref[pl.ds(k, PAD, stride=LOCAL), :]
    return jnp.concatenate([part, jnp.zeros((PAD, PAD - NODES), F32)], axis=1)


def field_at(ref, start):
    return jnp.concatenate(
        [
            ref[pl.ds(start, PAD, stride=2), :],
            ref[pl.ds(start + 1, PAD, stride=2), :],
        ],
        axis=1,
    )


def main_kernel(
    state_h,
    rhs_h,
    modal_ref,
    visc_ref,
    gain_h,
    inv_h,
    rc0_h,
    rc1_h,
    rc2_h,
    ru_h,
    gl_ref,
    st,
    rh,
    gs,
    iv,
    padm,
    tv,
    c,
    sens,
    edge,
    hk,
    hj,
    sm,
    z,
    p4,
    m4,
    zb,
    xb,
    u,
    load_sem,
    st_sem,
    rh_sem,
    hk_send,
    hk_recv,
    hj_send,
    hj_recv,
    c_send,
    c_recv,
    u_send,
    u_recv,
    z_sem,
    x_send,
    x_recv,
    own_sem,
):
    b = lax.axis_index("blk")
    e = lax.axis_index("elem")
    nb = lax.axis_size("blk")
    ne = lax.axis_size("elem")
    bx = b // 2
    bl = b % 2
    parts = LOCAL // PART
    part_rows = 2 * NODES * PART
    block_rows = NODES * LOCAL

    def load_part(source, target, sem, p):
        first = pl.multiple_of(p * part_rows, 8)
        return pltpu.make_async_copy(
            source.at[pl.ds(first, part_rows)], target.at[p, pl.ds(0, part_rows)], sem.at[p]
        )

    load_inv = pltpu.make_async_copy(inv_h, iv.at[pl.ds(0, block_rows)], load_sem.at[0])
    load_gain = pltpu.make_async_copy(gain_h, gs.at[pl.ds(0, block_rows)], load_sem.at[1])
    for p in range(parts):
        load_part(state_h, st, st_sem, p).start()
    for p in range(parts):
        load_part(rhs_h, rh, rh_sem, p).start()
    load_inv.start()
    load_gain.start()

    barrier = pltpu.get_barrier_semaphore()

    def greet(i, carry):
        pl.semaphore_signal(barrier, inc=1, device_id={"elem": (e + i) % ne}, device_id_type=MESH)
        return carry

    lax.fori_loop(1, ne, greet, 0)
    for d in (1, 2, 4, 6, 7):
        pl.semaphore_signal(barrier, inc=1, device_id={"blk": (b + d) % nb}, device_id_type=MESH)

    for p in range(parts):
        st[p, pl.ds(part_rows, 8), :] = jnp.zeros((8, PAD), F32)
        rh[p, pl.ds(part_rows, 8), :] = jnp.zeros((8, PAD), F32)
    tail = (PAD - NODES) * LOCAL
    gs[pl.ds(block_rows, tail), :] = jnp.zeros((tail, NODES), F32)
    iv[pl.ds(block_rows, tail), :] = jnp.zeros((tail, NODES), F32)

    padm[...] = jnp.zeros((2, PAD, PAD), F32)
    padm[0, 0:NODES, 0:NODES] = modal_ref[...]
    padm[1, 0:NODES, 0:NODES] = visc_ref[...]
    for i in range(2):
        tv[pl.ds(i * PAD, PAD), :] = as_rows(padm[i])

    def sense(source, within, k):
        both = product(tv[...], stacked(field_at(source, 2 * NODES * within)))
        c[k, 0] = both[PAD:, :PAD]
        c[k, 1] = both[PAD:, PAD:]
        squares = both[:PAD] * both[:PAD]
        low = jnp.sum(squares[: ORDER**3], axis=0, keepdims=True)
        upper = jnp.sum(squares[ORDER**3 :], axis=0, keepdims=True)
        value = (upper / NODES) / ((low + upper) / NODES + 1e-6)
        sens[0, pl.ds(k, 1), :] = value[:, :PAD]
        sens[1, pl.ds(k, 1), :] = value[:, PAD:]

    def sense_part(p, carry):
        load_part(state_h, st, st_sem, p).wait()

        def some(i, inner_carry):
            for r in range(UNROLL):
                sense(st.at[p], UNROLL * i + r, PART * p + UNROLL * i + r)
            return inner_carry

        lax.fori_loop(0, PART // UNROLL, some, 0)
        return carry

    lax.fori_loop(0, parts, sense_part, 0)
    for j in range(2):
        edge[0, j : j + 1, :] = sens[j, 0:1, :]
        edge[1, j : j + 1, :] = sens[j, LOCAL - 1 : LOCAL, :]
    pl.semaphore_wait(barrier, ne - 1 + 5)

    to_next = pltpu.make_async_remote_copy(
        edge.at[1], hk.at[0], hk_send.at[0], hk_recv.at[0],
        device_id={"blk": (b + 1) % nb}, device_id_type=MESH,
    )
    to_last = pltpu.make_async_remote_copy(
        edge.at[0], hk.at[1], hk_send.at[1], hk_recv.at[1],
        device_id={"blk": (b + nb - 1) % nb}, device_id_type=MESH,
    )
    outer = pltpu.make_async_remote_copy(
        sens.at[1], hj.at[0], hj_send.at[0], hj_recv.at[0],
        device_id={"elem": (e + 1) % ne}, device_id_type=MESH,
    )
    inner = pltpu.make_async_remote_copy(
        sens.at[0], hj.at[1], hj_send.at[1], hj_recv.at[1],
        device_id={"elem": (e + ne - 1) % ne}, device_id_type=MESH,
    )
    for copy in (outer, inner, to_next, to_last):
        copy.start()
    for copy in (outer, inner, to_next, to_last):
        copy.wait_recv()
    has_inner = jnp.where(e > 0, 1.0, 0.0).astype(F32)
    has_outer = jnp.where(e < ne - 1, 1.0, 0.0).astype(F32)
    beside = (hj[0] * has_inner, sens[0], sens[1], hj[1] * has_outer)
    for j in range(2):
        here = sens[j]
        before = jnp.concatenate([hk[0, j : j + 1, :], here[:-1]], axis=0)
        after = jnp.concatenate([here[1:], hk[1, j : j + 1, :]], axis=0)
        sm[j] = (4.0 * here + after + before + beside[j + 2] + beside[j]) / 8.0

    load_inv.wait()

    def wait_rhs(p, carry):
        load_part(rhs_h, rh, rh_sem, p).wait()
        return carry

    lax.fori_loop(0, parts, wait_rhs, 0)

    def force_one(k):
        scale = jnp.concatenate(
            [
                jnp.broadcast_to(sm[0, pl.ds(k, 1), :], (PAD, PAD)),
                jnp.broadcast_to(sm[1, pl.ds(k, 1), :], (PAD, PAD)),
            ],
            axis=1,
        )
        force = field_at(rh.at[k // PART], 2 * NODES * (k % PART)) + scale * jnp.concatenate([c[k, 0], c[k, 1]], axis=1)
        coupled = product(as_rows(block_of(iv, k)), stacked(force))
        c[k, 0] = coupled[:, :PAD]
        c[k, 1] = coupled[:, PAD:]

    rc_h = (rc0_h, rc1_h, rc2_h)

    def early_parts(to, source):
        return [
            pltpu.make_async_remote_copy(
                c.at[CHUNK * to + 1 + r], rc_h[r].at[source], c_send.at[r, to],
                c_recv.at[r, source], device_id={"elem": to}, device_id_type=MESH,
            )
            for r in range(CHUNK - 1)
        ]

    def early(to):
        for copy in early_parts(to, e):
            copy.start()

    side = ne // 2
    mine = side * (e // side)

    def near(d):
        return mine + (e + d) % side

    def far(d):
        return side - mine + (e + d) % side

    def forcing(to):
        for r in range(CHUNK):
            force_one(CHUNK * to + r)

    def force_both(d, carry):
        forcing(far(d))
        early(far(d))
        forcing(near(d + 1))
        early(near(d + 1))
        return carry

    def force_near(d, carry):
        forcing(near(d))
        early(near(d))
        return carry

    def force_far(d, carry):
        forcing(far(d))
        return carry

    def send_far(d, carry):
        early(far(d))
        return carry

    lax.fori_loop(0, HOLD, force_both, 0)
    lax.fori_loop(HOLD + 1, side, force_near, 0)
    lax.fori_loop(HOLD, side, force_far, 0)
    for r in range(CHUNK):
        force_one(CHUNK * e + r)
    own_c = [
        pltpu.make_async_copy(c.at[CHUNK * e + 1 + r], rc_h[r].at[e], own_sem.at[1 + r])
        for r in range(CHUNK - 1)
    ]
    for copy in own_c:
        copy.start()

    load_gain.wait()
    row = lax.broadcasted_iota(jnp.int32, (PAD, PAD), 0)
    column = lax.broadcasted_iota(jnp.int32, (PAD, PAD), 1)
    z[:, pl.ds(0, 2 * PAD)] = jnp.zeros((PAD, 2 * PAD), F32)
    z[:, pl.ds(2 * PAD, PAD)] = jnp.where((row == column) & (row < NODES), 1.0, 0.0).astype(F32)

    def sweep(k):
        made = product(as_rows(block_of(gs, k)), stacked(z[...]))
        z[:, pl.ds(0, PAD)] = made[:, :PAD] + c[k, 0]
        z[:, pl.ds(PAD, PAD)] = made[:, PAD : 2 * PAD] + c[k, 1]
        z[:, pl.ds(2 * PAD, PAD)] = made[:, 2 * PAD :]

    def sweeps(i, carry):
        for r in range(CHUNK):
            sweep(CHUNK * i + r)
            if r == 0:
                p4[i] = z[:, pl.ds(0, 2 * PAD)]
                m4[i] = as_rows(z[:, pl.ds(2 * PAD, PAD)])
        return carry

    lax.fori_loop(0, LOCAL // CHUNK, sweeps, 0)

    zb[bl] = z[...]
    pair = pltpu.make_async_remote_copy(
        zb.at[bl], zb.at[bl], z_sem.at[0], z_sem.at[1],
        device_id={"blk": b + 1 - 2 * bl}, device_id_type=MESH,
    )
    pair.start()
    lax.fori_loop(HOLD, side, send_far, 0)
    for i in range(CHUNK - 1):
        gl_ref[i] = as_rows(block_of(gs, CHUNK * e + 1 + i))
    pair.wait()

    def advance(ref, at, field):
        return product(as_rows(ref[at, :, pl.ds(2 * PAD, PAD)]), stacked(field))

    made = advance(zb, 1, zb[0])
    xb[bx, :, pl.ds(0, 2 * PAD)] = made[:, : 2 * PAD] + zb[1, :, pl.ds(0, 2 * PAD)]
    xb[bx, :, pl.ds(2 * PAD, PAD)] = made[:, 2 * PAD :]
    ring = nb // 2

    def along(i):
        return pltpu.make_async_remote_copy(
            xb.at[bx], xb.at[bx], x_send.at[i], x_recv.at[i],
            device_id={"blk": (b + 2 * i) % nb}, device_id_type=MESH,
        )

    for i in range(1, ring):
        along(i).start()
    for i in range(1, ring):
        along(i).wait()

    field = z.at[:, pl.ds(0, 2 * PAD)]
    field[...] = jnp.zeros((PAD, 2 * PAD), F32)

    def pass_pair(i, carry):
        at = i % ring
        field[...] = advance(xb, at, field[...]) + xb[at, :, pl.ds(0, 2 * PAD)]
        return carry

    lax.fori_loop(0, ring + bx, pass_pair, 0)

    @pl.when(bl == 1)
    def _():
        field[...] = advance(zb, 0, field[...]) + zb[0, :, pl.ds(0, 2 * PAD)]

    start = stacked(field[...])

    def late(to):
        return pltpu.make_async_remote_copy(
            u.at[to], ru_h.at[e], u_send.at[to], u_recv.at[e],
            device_id={"elem": to}, device_id_type=MESH,
        )

    def first_field(to):
        made = product(m4[to], start) + p4[to]
        u[to, 0] = made[:, :PAD]
        u[to, 1] = made[:, PAD:]

    def first_fields(i, carry):
        to = (e + ne // 2 + i - 1 + (i + ne // 2 - 1) // ne) % ne
        first_field(to)
        late(to).start()
        return carry

    lax.fori_loop(1, ne, first_fields, 0)
    first_field(e)
    own_u = pltpu.make_async_copy(u.at[e], ru_h.at[e], own_sem.at[0])
    own_u.start()
    for copy in own_c:
        copy.wait()
    own_u.wait()

    for copy in (outer, inner, to_next, to_last):
        copy.wait_send()

    def finish(i, carry):
        to = (e + i) % ne
        source = (e + ne - i) % ne
        late(to).wait_send()
        for copy in early_parts(to, e):
            copy.wait_send()
        for copy in early_parts(to, source):
            copy.wait_recv()
        pltpu.make_async_remote_copy(
            u.at[to], ru_h.at[source], u_send.at[to], u_recv.at[source],
            device_id={"elem": to}, device_id_type=MESH,
        ).wait_recv()
        return carry

    lax.fori_loop(1, ne, finish, 0)


def last_kernel(gl_ref, rc0_ref, rc1_ref, rc2_ref, ru_ref, out_ref):
    first = QUAD * pl.program_id(0)
    out = out_ref.reshape(CHUNK * NODES * 8, PAD)
    pairs = [(s, j) for s in range(QUAD) for j in range(2)]

    def put(r, field):
        for i in range(len(pairs)):
            out[pl.ds(r * NODES * 8 + i, NODES, stride=8), :] = field[
                :NODES, i * PAD : (i + 1) * PAD
            ]

    field = jnp.concatenate([ru_ref[first + s, j] for s, j in pairs], axis=1)
    put(0, field)
    for r, rc_ref in enumerate((rc0_ref, rc1_ref, rc2_ref)):
        source = jnp.concatenate([rc_ref[first + s, j] for s, j in pairs], axis=1)
        field = product(gl_ref[r], stacked(field)) + source
        put(r + 1, field)


def body(state, rhs, to_modal, viscous_op, sweep_gain, inv_blocks):
    ne = lax.axis_size("elem")
    rows = LOCAL * NODES * 2
    parts = LOCAL // PART
    flat = lambda x: x.reshape(rows, PAD)
    blocks = lambda x: jnp.transpose(x, (1, 0, 2)).reshape(NODES * LOCAL, NODES)
    vmem, dma = pltpu.VMEM, pltpu.SemaphoreType.DMA
    anywhere = pl.BlockSpec(memory_space=pl.ANY)
    far_memory = pl.BlockSpec(memory_space=pltpu.HBM)
    local = pl.BlockSpec(memory_space=pltpu.VMEM)
    blocks_in = jax.ShapeDtypeStruct((ne, 2, PAD, PAD), F32)
    rc0, rc1, rc2, ru, gl = pl.pallas_call(
        main_kernel,
        out_shape=(
            blocks_in,
            blocks_in,
            blocks_in,
            blocks_in,
            jax.ShapeDtypeStruct((CHUNK - 1, PAD, 3 * PAD), BF16),
        ),
        in_specs=[far_memory, far_memory, local, local, far_memory, far_memory],
        out_specs=(anywhere, anywhere, anywhere, anywhere, local),
        scratch_shapes=[
            vmem((parts, rows // parts + 8, PAD), F32),
            vmem((parts, rows // parts + 8, PAD), F32),
            vmem((PAD * LOCAL, NODES), F32),
            vmem((PAD * LOCAL, NODES), F32),
            vmem((2, PAD, PAD), F32),
            vmem((2 * PAD, 3 * PAD), BF16),
            vmem((LOCAL, 2, PAD, PAD), F32),
            vmem((2, LOCAL, PAD), F32),
            vmem((2, 8, PAD), F32),
            vmem((2, 8, PAD), F32),
            vmem((2, LOCAL, PAD), F32),
            vmem((2, LOCAL, PAD), F32),
            vmem((PAD, 3 * PAD), F32),
            vmem((LOCAL // CHUNK, PAD, 2 * PAD), F32),
            vmem((LOCAL // CHUNK, PAD, 3 * PAD), BF16),
            vmem((2, PAD, 3 * PAD), F32),
            vmem((4, PAD, 3 * PAD), F32),
            vmem((LOCAL // CHUNK, 2, PAD, PAD), F32),
            dma((2,)),
            dma((parts,)),
            dma((parts,)),
            dma((2,)),
            dma((2,)),
            dma((2,)),
            dma((2,)),
            dma((CHUNK - 1, 16)),
            dma((CHUNK - 1, 16)),
            dma((16,)),
            dma((16,)),
            dma((2,)),
            dma((4,)),
            dma((4,)),
            dma((CHUNK,)),
        ],
        compiler_params=pltpu.CompilerParams(
            collective_id=0, has_side_effects=True, vmem_limit_bytes=42 * 2**20
        ),
        name="line_main",
    )(flat(state), flat(rhs), to_modal, viscous_op, blocks(sweep_gain), blocks(inv_blocks))
    out = pl.pallas_call(
        last_kernel,
        grid=(ne // QUAD,),
        out_shape=jax.ShapeDtypeStruct((CHUNK * NODES, 2 * ne, PAD), F32),
        in_specs=[local] * 5,
        out_specs=pl.BlockSpec((CHUNK * NODES, 8, PAD), lambda i: (0, i, 0)),
        compiler_params=pltpu.CompilerParams(vmem_limit_bytes=40 * 2**20),
        name="line_last",
    )(gl, rc0, rc1, rc2, ru)
    return out.reshape(CHUNK, NODES, 2 * ne, PAD)


def solution(mesh):
    in_specs = (
        P("blk", None, "elem", None),
        P("blk", None, "elem", None),
        P(),
        P(),
        P("blk", None, None),
        P("blk", None, None),
    )
    out_specs = P(("blk", "elem"), None, None, None)
    return jax.shard_map(body, mesh=mesh, in_specs=in_specs, out_specs=out_specs, check_vma=False)
```
